512 devices in a mesh: ctx: 32 (over y, z_lo, core), layer: 16 (over z_hi, x).
Axes of the slice: x: 4, y: 4, z: 16 (z_hi: 4, z_lo: 4; z = z_hi * 4 + z_lo), core: 2. Of those that a mesh axis runs over, the one named last changes fastest.
Arguments:
- acts: bfloat16 [16, 4096, 8192], P('layer', 'ctx'), may hold values from -6 to 6
- grads_out: bfloat16 [16, 4096, 8192], P('layer', 'ctx'), may hold values from -6 to 6
- proj_in: bfloat16 [16, 8192, 128], P('layer', 'ctx'), may hold values from -0.0625 to 0.0625
- proj_out: bfloat16 [16, 8192, 128], P('layer', 'ctx'), may hold values from -0.0625 to 0.0625
- basis_a: float32 [16, 128, 128], P('layer'), may hold values from -1 to 1, as said below
- basis_g: float32 [16, 128, 128], P('layer'), may hold values from -1 to 1, as said below
- eig_a: float32 [16, 128], P('layer'), may hold values from 0.3 to 3
- eig_g: float32 [16, 128], P('layer'), may hold values from 0.3 to 3
- train_grads: bfloat16 [16, 512, 16384], P('layer', 'ctx'), may hold values from -0.75 to 0.75
Outputs:
- scores: float32 [512], P('ctx')
The draws below stay inside these ranges and needn't reach their ends.
Inputs may be any that keep to these rules, and one draw needn't show every extreme that they name: Each basis_a[l] is an orthogonal matrix up to float32 rounding. Each basis_g[l] is an orthogonal matrix up to float32 rounding.
All inputs are finite; a program needn't handle non-finite values.
Results may differ from the reference program's by a relative error of at most 0.0051.
Values may be sent and summed in bfloat16 or wider, within the bound.
No kernel may reach another device: no remote copies, remote signals or barrier semaphores. Data moves between devices by JAX's collectives and lax.ppermute only.
A program may use at most 64 MiB of HBM per device.

```python
import math
import jax
import jax.numpy as jnp
from jax import lax

D = 8192
R = 128
NTRAIN = 512
TOK_DEV = 128
TOKENS = 4096
LAYERS = 16
N_CTX = 32


def orthogonal_stack(key):
    matrix = jax.random.normal(key, (LAYERS, R, R), jnp.float32)
    factor, upper = jnp.linalg.qr(matrix)
    return factor.astype(jnp.float32)


def draw_basis_a(key, part):
    return orthogonal_stack(jax.random.fold_in(key, 11))


def draw_basis_g(key, part):
    return orthogonal_stack(jax.random.fold_in(key, 12))


def block_levels(own_key, extent, split, smallest, top_value):
    def one(position, shards_of):
        heights = jax.random.uniform(jax.random.fold_in(jax.random.fold_in(own_key, 6), position), (shards_of,), jnp.float32, smallest / len(split), top_value / len(split))
        return jnp.repeat(jnp.exp(heights), extent[position] // shards_of).reshape((-1,) + (1,) * (len(extent) - position - 1))

    level = one(*split[0])
    for cut in split[1:]:
        level = level * one(*cut)
    return level


def centred(own_key, shape, spread, most, pieces=(), held_as=jnp.bfloat16):
    array = jax.random.normal(own_key, shape, jnp.float32) * spread
    if len(pieces) > 0:
        array = block_levels(own_key, shape, pieces, -0.22, 0.18) * array
    return jnp.clip(array, min=-most, max=most).astype(held_as)


def setup_inputs(seed: int = 0) -> dict:
    key_of = jax.random.split(jax.random.key(seed), 10)
    return {
        "acts": centred(key_of[0], (LAYERS, TOKENS, D), 1.0, 6.0, ((0, 16), (1, 32))),
        "grads_out": centred(key_of[1], (LAYERS, TOKENS, D), 1.0, 6.0, ((0, 16), (1, 32))),
        "proj_in": centred(key_of[2], (LAYERS, D, R), D ** -0.5, 0.0625, ((0, 16), (1, 32))),
        "proj_out": centred(key_of[3], (LAYERS, D, R), D ** -0.5, 0.0625, ((0, 16), (1, 32))),
        "basis_a": draw_basis_a(jax.random.fold_in(key_of[9], 71), 0),
        "basis_g": draw_basis_g(jax.random.fold_in(key_of[9], 71), 0),
        "eig_a": jnp.clip(jnp.exp(math.log(3.0) - 2.3025851 * jax.random.uniform(key_of[6], (LAYERS, R), jnp.float32) ** block_levels(key_of[6], (LAYERS, R), ((0, 16),), -0.2, 0.2)), 0.3, 3.0),
        "eig_g": jnp.clip(jnp.exp(math.log(3.0) - 2.3025851 * jax.random.uniform(key_of[7], (LAYERS, R), jnp.float32) ** block_levels(key_of[7], (LAYERS, R), ((0, 16),), -0.2, 0.2)), 0.3, 3.0),
        "train_grads": centred(key_of[8], (LAYERS, NTRAIN, R * R), (R * R * LAYERS // (TOK_DEV * N_CTX)) ** -0.5, 0.75, ((0, 16), (1, 32))),
    }


def one_layer(items):
    acts, grads_out, proj_in, proj_out, basis_a, basis_g, eig_a, eig_g, train_grads = items
    proj_acts = jnp.dot(acts.astype(jnp.float32), proj_in.astype(jnp.float32), preferred_element_type=jnp.float32).astype(jnp.bfloat16)
    proj_grads = jnp.dot(grads_out.astype(jnp.float32), proj_out.astype(jnp.float32), preferred_element_type=jnp.float32).astype(jnp.bfloat16)
    doc_gradient = jnp.dot(proj_grads.T.astype(jnp.float32), proj_acts.astype(jnp.float32), preferred_element_type=jnp.float32) / TOKENS
    rotated = jnp.dot(jnp.dot(basis_g.T, doc_gradient, precision=lax.Precision.HIGHEST), basis_a, precision=lax.Precision.HIGHEST)
    whitened = rotated / (eig_g[:, None] * eig_a[None, :])
    precond = jnp.dot(jnp.dot(basis_g, whitened, precision=lax.Precision.HIGHEST), basis_a.T, precision=lax.Precision.HIGHEST)
    precond = precond.astype(jnp.bfloat16)
    return jnp.dot(train_grads.astype(jnp.float32), precond.reshape(-1).astype(jnp.float32), preferred_element_type=jnp.float32)

def reference(acts, grads_out, proj_in, proj_out, basis_a, basis_g, eig_a, eig_g, train_grads):
    per_layer = lax.map(one_layer, (acts, grads_out, proj_in, proj_out, basis_a, basis_g, eig_a, eig_g, train_grads))
    return jnp.sum(per_layer, axis=0)
```

```python
import functools

import jax
import jax.numpy as jnp
from jax import lax
from jax.experimental import pallas as pl
from jax.experimental.pallas import tpu as pltpu
from jax.sharding import Mesh, PartitionSpec as P

F32 = jnp.float32
BF16 = jnp.bfloat16
HIGHEST = lax.Precision.HIGHEST

CTX = ("y", "zlo", "core")
LAYER = ("zhi", "x")
VMEM = pl.BlockSpec(memory_space=pltpu.VMEM)
SMEM = pl.BlockSpec(memory_space=pltpu.SMEM)


def half_products(parity, acts_ref, grads_ref, rows_ref, acc_a, acc_g):
    blocks, _, depth, _ = rows_ref.shape
    for b in range(blocks):
        start = pl.multiple_of((2 * b + parity) * depth, depth)
        cols = pl.ds(start, depth)
        acc_a = acc_a + jnp.dot(acts_ref[:, cols], rows_ref[b, 0], preferred_element_type=F32)
        acc_g = acc_g + jnp.dot(grads_ref[:, cols], rows_ref[b, 1], preferred_element_type=F32)
    return acc_a, acc_g


def first_half(core_ref, acts_ref, grads_ref, rows_ref, out_a, out_g):
    zero = jnp.zeros(out_a.shape, F32)
    out_a[...], out_g[...] = half_products(core_ref[0], acts_ref, grads_ref, rows_ref, zero, zero)


def second_half(tokens, core_ref, acts_ref, grads_ref, rows_ref, in_a, in_g, out):
    acc_a, acc_g = half_products(
        1 - core_ref[0], acts_ref, grads_ref, rows_ref, in_a[...], in_g[...]
    )
    proj_a, proj_g = acc_a.astype(BF16), acc_g.astype(BF16)
    outer = lax.dot_general(
        proj_g, proj_a, (((0,), (0,)), ((), ())), preferred_element_type=F32
    )
    out[...] = outer / tokens


def score(parts_ref, basis_a, basis_g, eig_a, eig_g, train_ref, out):
    grad = parts_ref[0]
    for k in range(1, parts_ref.shape[0]):
        grad = grad + parts_ref[k]
    rot_a, rot_g = basis_a[...], basis_g[...]
    dot = functools.partial(
        lax.dot_general, precision=HIGHEST, preferred_element_type=F32
    )
    nn, tn, nt = (((1,), (0,)), ((), ())), (((0,), (0,)), ((), ())), (((1,), (1,)), ((), ()))
    turned = dot(dot(rot_g, grad, tn), rot_a, nn)
    rank = turned.shape[0]
    eye = (
        lax.broadcasted_iota(jnp.int32, (rank, rank), 0)
        == lax.broadcasted_iota(jnp.int32, (rank, rank), 1)
    )
    row_eig = jnp.sum(jnp.where(eye, jnp.broadcast_to(eig_g[...], (rank, rank)), 0.0), 1, keepdims=True)
    whitened = turned / (row_eig * eig_a[...])
    precond = dot(dot(rot_g, whitened, nn), rot_a, nt).astype(BF16).astype(F32)
    total = jnp.zeros((train_ref.shape[0], rank), F32)
    for i in range(rank):
        total = total + train_ref[:, i * rank:(i + 1) * rank].astype(F32) * precond[i:i + 1, :]
    out[...] = dot(jnp.ones((out.shape[0], rank), F32), total, nt)


def to_all(x, axis):
    size = lax.axis_size(axis)
    return lax.all_to_all(jnp.broadcast_to(x, (size,) + x.shape), axis, 0, 0)


def body(acts, grads_out, proj_in, proj_out, basis_a, basis_g, eig_a, eig_g, train_grads):
    tokens = acts.shape[1] * lax.axis_size(CTX)
    n_layer = lax.axis_size(LAYER)
    rank = proj_in.shape[-1]
    depth = proj_in.shape[1]
    swap = [(0, 1), (1, 0)]
    core = lax.axis_index("core").astype(jnp.int32).reshape(1)
    acts2, grads2 = acts[0], grads_out[0]
    n_tok = acts2.shape[0]

    mine = jnp.concatenate([proj_in, proj_out], 0)
    rows = to_all(to_all(mine, "zlo"), "y").reshape(-1, 2, depth, rank)
    theirs = lax.ppermute(rows, "core", swap)

    small = jax.ShapeDtypeStruct((n_tok, rank), F32)
    flops = 2 * n_tok * acts2.shape[1] * rank
    cost = pl.CostEstimate(flops=flops, bytes_accessed=6 << 20, transcendentals=0)
    acc = pl.pallas_call(
        first_half,
        out_shape=(small, small),
        in_specs=[SMEM, VMEM, VMEM, VMEM],
        out_specs=(VMEM, VMEM),
        cost_estimate=cost,
        name="first_half",
    )(core, acts2, grads2, rows)
    grad = pl.pallas_call(
        functools.partial(second_half, float(tokens)),
        out_shape=jax.ShapeDtypeStruct((rank, rank), F32),
        in_specs=[SMEM] + [VMEM] * 5,
        out_specs=VMEM,
        cost_estimate=cost,
        name="second_half",
    )(core, acts2, grads2, theirs, *acc)

    grad = grad + lax.ppermute(grad, "core", swap)
    grad = jnp.sum(to_all(grad, "y"), 0)
    parts = to_all(grad, "zlo")
    sent = pl.pallas_call(
        score,
        out_shape=jax.ShapeDtypeStruct((n_layer, train_grads.shape[1]), F32),
        in_specs=[VMEM] * 6,
        out_specs=VMEM,
        name="score",
    )(parts, basis_a[0], basis_g[0], eig_a, eig_g, train_grads[0])
    return jnp.sum(lax.all_to_all(sent, LAYER, 0, 0), 0)


def solution(mesh):
    devices = mesh.devices.reshape(4, 4, 2, 4, 4)
    fine = Mesh(devices, CTX + LAYER)
    return jax.shard_map(
        body,
        mesh=fine,
        in_specs=(
            P(LAYER, CTX, None),
            P(LAYER, CTX, None),
            P(LAYER, CTX, None),
            P(LAYER, CTX, None),
            P(LAYER, None, None),
            P(LAYER, None, None),
            P(LAYER, None),
            P(LAYER, None),
            P(LAYER, CTX, None),
        ),
        out_specs=P(CTX),
        check_vma=False,
    )
```

```python
import functools

import jax
import jax.numpy as jnp
from jax import lax
from jax.experimental import pallas as pl
from jax.experimental.pallas import tpu as pltpu
from jax.sharding import Mesh, PartitionSpec as P


F32 = jnp.float32
BF16 = jnp.bfloat16
HIGHEST = lax.Precision.HIGHEST

CTX = ("y", "zlo", "core")
LAYER = ("zhi", "x")
VMEM = pl.BlockSpec(memory_space=pltpu.VMEM)
SMEM = pl.BlockSpec(memory_space=pltpu.SMEM)


def products(pieces, here_ref, acts_ref, grads_ref, row_refs, acc_a, acc_g):
    n_y, n_z = here_ref[2], here_ref[3]
    for (blocks, flip), rows_ref in zip(pieces, row_refs):
        depth = rows_ref.shape[2]
        core = 1 - here_ref[1] if flip else here_ref[1]
        for k, (step, z) in enumerate(blocks):
            line = lax.rem(here_ref[0] + step, n_y) * n_z
            start = pl.multiple_of(((line + z) * 2 + core) * depth, depth)
            cols = pl.ds(start, depth)
            acc_a = acc_a + jnp.dot(acts_ref[:, cols], rows_ref[k, 0], preferred_element_type=F32)
            acc_g = acc_g + jnp.dot(grads_ref[:, cols], rows_ref[k, 1], preferred_element_type=F32)
    return acc_a, acc_g


def begin(pieces, here_ref, acts_ref, grads_ref, *refs):
    rows, (out_a, out_g) = refs[:-2], refs[-2:]
    zero = jnp.zeros(out_a.shape, F32)
    out_a[...], out_g[...] = products(pieces, here_ref, acts_ref, grads_ref, rows, zero, zero)


def go_on(pieces, here_ref, acts_ref, grads_ref, *refs):
    rows, (in_a, in_g, out_a, out_g) = refs[:-4], refs[-4:]
    out_a[...], out_g[...] = products(
        pieces, here_ref, acts_ref, grads_ref, rows, in_a[...], in_g[...]
    )


def finish(tokens, pieces, here_ref, acts_ref, grads_ref, *refs):
    rows, (in_a, in_g, out) = refs[:-3], refs[-3:]
    acc_a, acc_g = products(pieces, here_ref, acts_ref, grads_ref, rows, in_a[...], in_g[...])
    proj_a, proj_g = acc_a.astype(BF16), acc_g.astype(BF16)
    outer = lax.dot_general(
        proj_g, proj_a, (((0,), (0,)), ((), ())), preferred_element_type=F32
    )
    out[...] = outer / tokens


def score(parts_ref, basis_a, basis_g, eig_a, eig_g, train_ref, out):
    grad = parts_ref[0]
    for k in range(1, parts_ref.shape[0]):
        grad = grad + parts_ref[k]
    rot_a, rot_g = basis_a[...], basis_g[...]
    dot = functools.partial(
        lax.dot_general, precision=HIGHEST, preferred_element_type=F32
    )
    nn, tn, nt = (((1,), (0,)), ((), ())), (((0,), (0,)), ((), ())), (((1,), (1,)), ((), ()))
    turned = dot(dot(rot_g, grad, tn), rot_a, nn)
    rank = turned.shape[0]
    eye = (
        lax.broadcasted_iota(jnp.int32, (rank, rank), 0)
        == lax.broadcasted_iota(jnp.int32, (rank, rank), 1)
    )
    row_eig = jnp.sum(jnp.where(eye, jnp.broadcast_to(eig_g[...], (rank, rank)), 0.0), 1, keepdims=True)
    whitened = turned / (row_eig * eig_a[...])
    precond = dot(dot(rot_g, whitened, nn), rot_a, nt).astype(BF16).astype(F32)
    total = jnp.zeros((train_ref.shape[0], rank), F32)
    for i in range(rank):
        total = total + train_ref[:, i * rank:(i + 1) * rank].astype(F32) * precond[i:i + 1, :]
    out[...] = dot(jnp.ones((out.shape[0], rank), F32), total, nt)


def to_all(x, axis):
    size = lax.axis_size(axis)
    return lax.all_to_all(jnp.broadcast_to(x, (size,) + x.shape), axis, 0, 0)


def ring(size, step):
    return [(i, (i + step) % size) for i in range(size)]


def body(acts, grads_out, proj_in, proj_out, basis_a, basis_g, eig_a, eig_g, train_grads):
    tokens = acts.shape[1] * lax.axis_size(CTX)
    n_layer = lax.axis_size(LAYER)
    n_y, n_z = lax.axis_size("y"), lax.axis_size("zlo")
    rank = proj_in.shape[-1]
    half = n_z // 2
    acts2, grads2 = acts[0], grads_out[0]
    n_tok = acts2.shape[0]
    here = jnp.stack(
        [lax.axis_index("y"), lax.axis_index("core"), jnp.int32(n_y), jnp.int32(n_z)]
    ).astype(jnp.int32)

    def up(x):
        return lax.ppermute(x, "y", ring(n_y, 1))

    def down(x):
        return lax.ppermute(x, "y", ring(n_y, -1))

    def swap(x):
        return lax.ppermute(x, "core", ring(2, 1))

    def call(kernel, rows, acc, out_shape):
        count = sum(r.shape[0] for r in rows)
        flops = 4 * n_tok * count * rows[0].shape[2] * rank
        return pl.pallas_call(
            kernel,
            out_shape=out_shape,
            in_specs=[SMEM] + [VMEM] * (2 + len(rows) + len(acc)),
            out_specs=jax.tree.map(lambda _: VMEM, out_shape),
            cost_estimate=pl.CostEstimate(flops=flops, bytes_accessed=count << 17, transcendentals=0),
            compiler_params=pltpu.CompilerParams(vmem_limit_bytes=20 << 20),
        )(here, acts2, grads2, *rows, *acc)

    mine = jnp.concatenate([proj_in, proj_out], 0)
    line = to_all(mine, "zlo")
    low, high = line[:half], line[half:]
    from_below_low = up(low)
    from_above_high = down(high)
    from_below_high = up(high)
    from_above_low = down(low)
    other_line = swap(line)
    far_low = up(from_below_low)
    far_high = down(from_above_high)
    near = jnp.concatenate([from_below_low, from_below_high, from_above_low, from_above_high], 0)
    other_near = swap(near)
    far = jnp.concatenate([far_low, far_high], 0)
    other_far = swap(far)

    def row(step):
        return [(step, z) for z in range(n_z)]

    below, above, opposite = n_y - 1, 1, n_y // 2
    small = jax.ShapeDtypeStruct((n_tok, rank), F32)
    acc = call(
        functools.partial(begin, [
            (row(0), False),
            (row(below)[:half], False),
            (row(below)[half:], False),
            (row(above)[:half], False),
            (row(above)[half:], False),
        ]),
        [line, from_below_low, from_below_high, from_above_low, from_above_high],
        (), (small, small),
    )
    acc = call(
        functools.partial(go_on, [
            (row(0), True),
            (row(below) + row(above), True),
            (row(opposite), False),
        ]),
        [other_line, other_near, far], acc, (small, small),
    )
    grad = call(
        functools.partial(finish, float(tokens), [(row(opposite), True)]),
        [other_far], acc, jax.ShapeDtypeStruct((rank, rank), F32),
    )

    grad = grad + swap(grad)
    grad = jnp.sum(to_all(grad, "y"), 0)
    parts = to_all(grad, "zlo")
    sent = pl.pallas_call(
        score,
        out_shape=jax.ShapeDtypeStruct((n_layer, train_grads.shape[1]), F32),
        in_specs=[VMEM] * 6,
        out_specs=VMEM,
        compiler_params=pltpu.CompilerParams(vmem_limit_bytes=20 << 20),
        name="score",
    )(parts, basis_a[0], basis_g[0], eig_a, eig_g, train_grads[0])
    return jnp.sum(lax.all_to_all(sent, LAYER, 0, 0), 0)


def solution(mesh):
    devices = mesh.devices.reshape(4, 4, 2, 4, 4)
    fine = Mesh(devices, CTX + LAYER)
    return jax.shard_map(
        body,
        mesh=fine,
        in_specs=(
            P(LAYER, CTX, None),
            P(LAYER, CTX, None),
            P(LAYER, CTX, None),
            P(LAYER, CTX, None),
            P(LAYER, None, None),
            P(LAYER, None, None),
            P(LAYER, None),
            P(LAYER, None),
            P(LAYER, CTX, None),
        ),
        out_specs=P(CTX),
        check_vma=False,
    )
```

```python
import functools

import jax
import jax.numpy as jnp
from jax import lax
from jax.experimental import pallas as pl
from jax.experimental.pallas import tpu as pltpu
from jax.sharding import Mesh, PartitionSpec as P

F32 = jnp.float32
BF16 = jnp.bfloat16
HIGHEST = lax.Precision.HIGHEST

CTX = ("y", "zlo", "core")
LAYER = ("zhi", "x")
VMEM = pl.BlockSpec(memory_space=pltpu.VMEM)
SMEM = pl.BlockSpec(memory_space=pltpu.SMEM)


def deal(core_ref, acts_ref, grads_ref, keep_ref, send_ref, sems):
    def copies(keep_from, send_from):
        one = pltpu.make_async_copy(send_from, send_ref, sems.at[0])
        two = pltpu.make_async_copy(keep_from, keep_ref, sems.at[1])
        one.start()
        two.start()
        one.wait()
        two.wait()

    @pl.when(core_ref[0] == 0)
    def _():
        copies(acts_ref, grads_ref)

    @pl.when(core_ref[0] != 0)
    def _():
        copies(grads_ref, acts_ref)


def project(keep_ref, got_ref, rows_ref, out):
    depth = rows_ref.shape[1]
    n_tok = keep_ref.shape[0]
    mine = jnp.zeros((n_tok, rows_ref.shape[2]), F32)
    other = mine
    for b in range(rows_ref.shape[0]):
        cols = pl.ds(b * depth, depth)
        mine = mine + jnp.dot(keep_ref[:, cols], rows_ref[b], preferred_element_type=F32)
        other = other + jnp.dot(got_ref[:, cols], rows_ref[b], preferred_element_type=F32)
    out[0] = mine.astype(BF16)
    out[1] = other.astype(BF16)


def outer(tokens, core_ref, mine_ref, got_ref, out):
    even = core_ref[0] == 0
    total = jnp.zeros(out.shape[1:], F32)
    for k in range(2):
        mine, got = mine_ref[k].astype(F32), got_ref[1 - k].astype(F32)
        proj_g = jnp.where(even, got, mine).astype(BF16)
        proj_a = jnp.where(even, mine, got).astype(BF16)
        total = total + lax.dot_general(
            proj_g, proj_a, (((0,), (0,)), ((), ())), preferred_element_type=F32
        )
    total = total / tokens
    for k in range(out.shape[0]):
        out[k] = total


def score(parts_ref, basis_a, basis_g, eig_a, eig_g, train_ref, out):
    grad = parts_ref[0]
    for k in range(1, parts_ref.shape[0]):
        grad = grad + parts_ref[k]
    rot_a, rot_g = basis_a[...], basis_g[...]
    dot = functools.partial(
        lax.dot_general, precision=HIGHEST, preferred_element_type=F32
    )
    nn, tn, nt = (((1,), (0,)), ((), ())), (((0,), (0,)), ((), ())), (((1,), (1,)), ((), ()))
    turned = dot(dot(rot_g, grad, tn), rot_a, nn)
    rank = turned.shape[0]
    eye = (
        lax.broadcasted_iota(jnp.int32, (rank, rank), 0)
        == lax.broadcasted_iota(jnp.int32, (rank, rank), 1)
    )
    row_eig = jnp.sum(jnp.where(eye, jnp.broadcast_to(eig_g[...], (rank, rank)), 0.0), 1, keepdims=True)
    whitened = turned / (row_eig * eig_a[...])
    precond = dot(dot(rot_g, whitened, nn), rot_a, nt).astype(BF16).astype(F32)
    total = jnp.zeros((train_ref.shape[0], rank), F32)
    for i in range(rank):
        total = total + train_ref[:, i * rank:(i + 1) * rank].astype(F32) * precond[i:i + 1, :]
    out[...] = dot(jnp.ones((out.shape[0], rank), F32), total, nt)


def to_all(x, axis):
    size = lax.axis_size(axis)
    return lax.all_to_all(jnp.broadcast_to(x, (size,) + x.shape), axis, 0, 0)


def body(acts, grads_out, proj_in, proj_out, basis_a, basis_g, eig_a, eig_g, train_grads):
    tokens = acts.shape[1] * lax.axis_size(CTX)
    n_layer, n_y = lax.axis_size(LAYER), lax.axis_size("y")
    depth, rank = proj_in.shape[1:]
    core = lax.axis_index("core").astype(jnp.int32).reshape(1)
    local = acts[0]
    n_tok = local.shape[0]
    params = pltpu.CompilerParams(vmem_limit_bytes=20 << 20)

    def swap(x):
        return lax.ppermute(x, "core", [(0, 1), (1, 0)])

    piece = jax.ShapeDtypeStruct(local.shape, BF16)
    keep, send = pl.pallas_call(
        deal,
        out_shape=(piece, piece),
        in_specs=[SMEM, pl.BlockSpec(memory_space=pl.ANY), pl.BlockSpec(memory_space=pl.ANY)],
        out_specs=(VMEM, VMEM),
        scratch_shapes=[pltpu.SemaphoreType.DMA((2,))],
        compiler_params=params,
        name="deal",
    )(core, local, grads_out[0])
    got = swap(send)

    both = jnp.concatenate([proj_in, proj_out], 0)
    both = jnp.broadcast_to(both, (lax.axis_size("zlo"),) + both.shape)
    line = lax.all_to_all(both.reshape(-1, depth, rank), ("zlo", "core"), 0, 0, tiled=True)
    rows = to_all(line, "y").reshape(-1, depth, rank)

    mine = pl.pallas_call(
        project,
        out_shape=jax.ShapeDtypeStruct((2, n_tok, rank), BF16),
        in_specs=[VMEM] * 3,
        out_specs=VMEM,
        compiler_params=params,
        name="project",
    )(keep, got, rows)
    grad = pl.pallas_call(
        functools.partial(outer, float(tokens)),
        out_shape=jax.ShapeDtypeStruct((n_y, rank, rank), F32),
        in_specs=[SMEM, VMEM, VMEM],
        out_specs=VMEM,
        compiler_params=params,
        name="outer",
    )(core, mine, swap(mine))

    grad = jnp.sum(lax.all_to_all(grad, "y", 0, 0), 0)
    parts = to_all(grad, "zlo")
    sent = pl.pallas_call(
        score,
        out_shape=jax.ShapeDtypeStruct((n_layer, train_grads.shape[1]), F32),
        in_specs=[VMEM] * 6,
        out_specs=VMEM,
        compiler_params=params,
        name="score",
    )(parts, basis_a[0], basis_g[0], eig_a, eig_g, train_grads[0])
    return jnp.sum(lax.all_to_all(sent, LAYER, 0, 0), 0)


def solution(mesh):
    devices = mesh.devices.reshape(4, 4, 2, 4, 4)
    fine = Mesh(devices, CTX + LAYER)
    return jax.shard_map(
        body,
        mesh=fine,
        in_specs=(
            P(LAYER, CTX, None),
            P(LAYER, CTX, None),
            P(LAYER, CTX, None),
            P(LAYER, CTX, None),
            P(LAYER, None, None),
            P(LAYER, None, None),
            P(LAYER, None),
            P(LAYER, None),
            P(LAYER, CTX, None),
        ),
        out_specs=P(CTX),
        check_vma=False,
    )
```

```python
import functools

import jax
import jax.numpy as jnp
from jax import lax
from jax.experimental import pallas as pl
from jax.experimental.pallas import tpu as pltpu
from jax.sharding import Mesh, PartitionSpec as P


F32 = jnp.float32
BF16 = jnp.bfloat16
HIGHEST = lax.Precision.HIGHEST

CTX = ("y", "zlo", "core")
LAYER = ("zhi", "x")
VMEM = pl.BlockSpec(memory_space=pltpu.VMEM)
SMEM = pl.BlockSpec(memory_space=pltpu.SMEM)


def pack(in_ref, out_ref, out):
    for k in range(out.shape[0]):
        out[k, 0] = in_ref[...]
        out[k, 1] = out_ref[...]


def deal(here_ref, acts_ref, grads_ref, send_ref, sem):
    @pl.when(here_ref[1] == 0)
    def _():
        copy = pltpu.make_async_copy(grads_ref, send_ref, sem)
        copy.start()
        copy.wait()

    @pl.when(here_ref[1] != 0)
    def _():
        copy = pltpu.make_async_copy(acts_ref, send_ref, sem)
        copy.start()
        copy.wait()


def products(pieces, here_ref, acts_ref, grads_ref, got_ref, row_refs, mine, other):
    even = here_ref[1] == 0
    for (step, first), rows_ref in zip(pieces, row_refs):
        count, depth, _ = rows_ref.shape
        line = lax.rem(here_ref[0] + step, here_ref[2]) * here_ref[3]
        for k in range(count):
            cols = pl.ds(pl.multiple_of((line + (first + k)) * depth, depth), depth)
            keep = jnp.where(even, acts_ref[:, cols], grads_ref[:, cols])
            mine = mine + jnp.dot(keep, rows_ref[k], preferred_element_type=F32)
            other = other + jnp.dot(got_ref[:, cols], rows_ref[k], preferred_element_type=F32)
    return mine, other


def begin(pieces, here_ref, acts_ref, grads_ref, got_ref, *refs):
    rows, out = refs[:-1], refs[-1]
    zero = jnp.zeros(out.shape[1:], F32)
    out[0], out[1] = products(
        pieces, here_ref, acts_ref, grads_ref, got_ref, rows, zero, zero
    )


def finish(pieces, here_ref, acts_ref, grads_ref, got_ref, *refs):
    rows, (acc, out) = refs[:-2], refs[-2:]
    mine, other = products(
        pieces, here_ref, acts_ref, grads_ref, got_ref, rows, acc[0], acc[1]
    )
    out[0], out[1] = mine.astype(out.dtype), other.astype(out.dtype)


def outer(tokens, here_ref, mine_ref, got_ref, out):
    even = here_ref[1] == 0
    total = jnp.zeros(out.shape[1:], F32)
    for k in range(2):
        mine, got = mine_ref[k].astype(F32), got_ref[1 - k].astype(F32)
        proj_g = jnp.where(even, got, mine).astype(BF16)
        proj_a = jnp.where(even, mine, got).astype(BF16)
        total = total + lax.dot_general(
            proj_g, proj_a, (((0,), (0,)), ((), ())), preferred_element_type=F32
        )
    total = (total / tokens).astype(out.dtype)
    for k in range(out.shape[0]):
        out[k] = total


def add_up(parts_ref, out):
    total = parts_ref[0].astype(F32)
    for k in range(1, parts_ref.shape[0]):
        total = total + parts_ref[k].astype(F32)
    total = total.astype(out.dtype)
    for k in range(out.shape[0]):
        out[k] = total


def score(parts_ref, basis_a, basis_g, eig_a, eig_g, train_ref, out):
    grad = parts_ref[0].astype(F32)
    for k in range(1, parts_ref.shape[0]):
        grad = grad + parts_ref[k].astype(F32)
    rot_a, rot_g = basis_a[...], basis_g[...]
    dot = functools.partial(
        lax.dot_general, precision=HIGHEST, preferred_element_type=F32
    )
    nn, tn, nt = (((1,), (0,)), ((), ())), (((0,), (0,)), ((), ())), (((1,), (1,)), ((), ()))
    turned = dot(dot(rot_g, grad, tn), rot_a, nn)
    rank = turned.shape[0]
    eye = (
        lax.broadcasted_iota(jnp.int32, (rank, rank), 0)
        == lax.broadcasted_iota(jnp.int32, (rank, rank), 1)
    )
    row_eig = jnp.sum(jnp.where(eye, jnp.broadcast_to(eig_g[...], (rank, rank)), 0.0), 1, keepdims=True)
    whitened = turned / (row_eig * eig_a[...])
    precond = dot(dot(rot_g, whitened, nn), rot_a, nt).astype(BF16).astype(F32)
    total = jnp.zeros((train_ref.shape[0], rank), F32)
    for i in range(rank):
        total = total + train_ref[:, i * rank:(i + 1) * rank].astype(F32) * precond[i:i + 1, :]
    out[...] = dot(jnp.ones((out.shape[0], rank), F32), total, nt)


def body(acts, grads_out, proj_in, proj_out, basis_a, basis_g, eig_a, eig_g, train_grads):
    tokens = acts.shape[1] * lax.axis_size(CTX)
    n_layer = lax.axis_size(LAYER)
    n_y, n_z = lax.axis_size("y"), lax.axis_size("zlo")
    depth, rank = proj_in.shape[1:]
    line_blocks = 2 * n_z
    half = n_z
    local, local_g = acts[0], grads_out[0]
    n_tok = local.shape[0]
    hbm = pl.BlockSpec(memory_space=pltpu.HBM)
    here = jnp.stack(
        [lax.axis_index("y"), lax.axis_index("core"), jnp.int32(n_y), jnp.int32(line_blocks)]
    ).astype(jnp.int32)

    def call(kernel, shape, in_specs, *args, **more):
        return pl.pallas_call(
            kernel,
            out_shape=shape,
            in_specs=in_specs,
            out_specs=VMEM,
            compiler_params=pltpu.CompilerParams(vmem_limit_bytes=20 << 20),
            **more,
        )(*args)

    def shape(*dims, dtype=BF16):
        return jax.ShapeDtypeStruct(dims, dtype)

    def all_to_all(x, axis):
        return lax.all_to_all(x, axis, 0, 0, tiled=True)

    def permute(x, axis, step):
        size = lax.axis_size(axis)
        return lax.ppermute(x, axis, [(i, (i + step) % size) for i in range(size)])

    both = call(pack, shape(n_z, 2, depth, rank), [VMEM] * 2, proj_in[0], proj_out[0])
    line = all_to_all(both.reshape(line_blocks, depth, rank), ("zlo", "core"))
    send = call(
        deal, shape(*local.shape), [SMEM, hbm, hbm], here, local, local_g,
        scratch_shapes=[pltpu.SemaphoreType.DMA],
    )
    got = permute(send, "core", 1)

    low, high = line[:half], line[half:]
    below_low = permute(low, "y", 1)
    above_high = permute(high, "y", -1)
    below_high = permute(high, "y", 1)
    above_low = permute(low, "y", -1)
    far_low = permute(below_low, "y", 1)
    far_high = permute(above_high, "y", -1)

    below, above, far = n_y - 1, 1, n_y // 2
    near = {(0, 0): line, (below, 0): below_low, (below, half): below_high,
            (above, 0): above_low, (above, half): above_high}
    cost = pl.CostEstimate(
        flops=4 * n_tok * rank * local.shape[1] * 3 // 4, bytes_accessed=6 << 20, transcendentals=0
    )
    acc = call(
        functools.partial(begin, tuple(near)), shape(2, n_tok, rank, dtype=F32),
        [SMEM] + [VMEM] * (3 + len(near)),
        here, local, local_g, got, *near.values(), cost_estimate=cost,
    )
    mine = call(
        functools.partial(finish, ((far, 0), (far, half))), shape(2, n_tok, rank),
        [SMEM] + [VMEM] * 6,
        here, local, local_g, got, far_low, far_high, acc,
    )
    grad = call(
        functools.partial(outer, float(tokens)), shape(n_y, rank, rank),
        [SMEM, VMEM, VMEM], here, mine, permute(mine, "core", 1),
    )
    grad = call(add_up, shape(n_z, rank, rank), [VMEM], all_to_all(grad, "y"))
    sent = call(
        score, shape(n_layer, train_grads.shape[1], dtype=F32), [VMEM] * 6,
        all_to_all(grad, "zlo"), basis_a[0], basis_g[0], eig_a, eig_g, train_grads[0],
    )
    return jnp.sum(lax.all_to_all(sent, LAYER, 0, 0), 0)


def solution(mesh):
    devices = mesh.devices.reshape(4, 4, 2, 4, 4)
    fine = Mesh(devices, CTX + LAYER)
    return jax.shard_map(
        body,
        mesh=fine,
        in_specs=(
            P(LAYER, CTX, None),
            P(LAYER, CTX, None),
            P(LAYER, CTX, None),
            P(LAYER, CTX, None),
            P(LAYER, None, None),
            P(LAYER, None, None),
            P(LAYER, None),
            P(LAYER, None),
            P(LAYER, CTX, None),
        ),
        out_specs=P(CTX),
        check_vma=False,
    )
```

```python
import functools

import jax
import jax.numpy as jnp
from jax import lax
from jax.experimental import pallas as pl
from jax.experimental.pallas import tpu as pltpu
from jax.sharding import Mesh, PartitionSpec as P


F32 = jnp.float32
BF16 = jnp.bfloat16
HIGHEST = lax.Precision.HIGHEST

CTX = ("y", "zlo", "core")
LAYER = ("zhi", "x")
VMEM = pl.BlockSpec(memory_space=pltpu.VMEM)
SMEM = pl.BlockSpec(memory_space=pltpu.SMEM)


def pack(in_ref, out_ref, out):
    for k in range(out.shape[0]):
        out[k, 0] = in_ref[...]
        out[k, 1] = out_ref[...]


def deal(here_ref, acts_ref, grads_ref, send_ref, sem):
    @pl.when(here_ref[1] == 0)
    def _():
        copy = pltpu.make_async_copy(grads_ref, send_ref, sem)
        copy.start()
        copy.wait()

    @pl.when(here_ref[1] != 0)
    def _():
        copy = pltpu.make_async_copy(acts_ref, send_ref, sem)
        copy.start()
        copy.wait()


def products(pieces, here_ref, acts_ref, grads_ref, got_ref, row_refs, mine, other):
    even = here_ref[1] == 0
    for (step, first), rows_ref in zip(pieces, row_refs):
        count, depth, _ = rows_ref.shape
        line = lax.rem(here_ref[0] + step, here_ref[2]) * here_ref[3]
        for k in range(count):
            cols = pl.ds(pl.multiple_of((line + (first + k)) * depth, depth), depth)
            keep = jnp.where(even, acts_ref[:, cols], grads_ref[:, cols])
            mine = mine + jnp.dot(keep, rows_ref[k], preferred_element_type=F32)
            other = other + jnp.dot(got_ref[:, cols], rows_ref[k], preferred_element_type=F32)
    return mine, other


def begin(pieces, far, here_ref, acts_ref, grads_ref, got_ref, *refs):
    rows, (out, ahead) = refs[:-2], refs[-2:]
    zero = jnp.zeros(out.shape[1:], F32)
    out[0], out[1] = products(
        pieces, here_ref, acts_ref, grads_ref, got_ref, rows, zero, zero
    )
    width = ahead.shape[2]
    line = lax.rem(here_ref[0] + far, here_ref[2])
    cols = pl.ds(pl.multiple_of(line * width, width), width)
    ahead[0] = jnp.where(here_ref[1] == 0, acts_ref[:, cols], grads_ref[:, cols])
    ahead[1] = got_ref[:, cols]


def finish(ahead_ref, low_ref, high_ref, acc_ref, out):
    mine, other = acc_ref[0], acc_ref[1]
    depth = low_ref.shape[1]
    done = 0
    for rows_ref in (low_ref, high_ref):
        for k in range(rows_ref.shape[0]):
            cols = pl.ds((done + k) * depth, depth)
            mine = mine + jnp.dot(ahead_ref[0, :, cols], rows_ref[k], preferred_element_type=F32)
            other = other + jnp.dot(ahead_ref[1, :, cols], rows_ref[k], preferred_element_type=F32)
        done += rows_ref.shape[0]
    out[0], out[1] = mine.astype(out.dtype), other.astype(out.dtype)


def outer(tokens, here_ref, mine_ref, got_ref, out):
    even = here_ref[1] == 0
    total = jnp.zeros(out.shape[1:], F32)
    for k in range(2):
        mine, got = mine_ref[k].astype(F32), got_ref[1 - k].astype(F32)
        proj_g = jnp.where(even, got, mine).astype(BF16)
        proj_a = jnp.where(even, mine, got).astype(BF16)
        total = total + lax.dot_general(
            proj_g, proj_a, (((0,), (0,)), ((), ())), preferred_element_type=F32
        )
    total = (total / tokens).astype(out.dtype)
    for k in range(out.shape[0]):
        out[k] = total


def add_up(parts_ref, out):
    total = parts_ref[0].astype(F32)
    for k in range(1, parts_ref.shape[0]):
        total = total + parts_ref[k].astype(F32)
    total = total.astype(out.dtype)
    for k in range(out.shape[0]):
        out[k] = total


def score(parts_ref, basis_a, basis_g, eig_a, eig_g, train_ref, out):
    grad = parts_ref[0].astype(F32)
    for k in range(1, parts_ref.shape[0]):
        grad = grad + parts_ref[k].astype(F32)
    rot_a, rot_g = basis_a[...], basis_g[...]
    dot = functools.partial(
        lax.dot_general, precision=HIGHEST, preferred_element_type=F32
    )
    nn, tn, nt = (((1,), (0,)), ((), ())), (((0,), (0,)), ((), ())), (((1,), (1,)), ((), ()))
    turned = dot(dot(rot_g, grad, tn), rot_a, nn)
    rank = turned.shape[0]
    eye = (
        lax.broadcasted_iota(jnp.int32, (rank, rank), 0)
        == lax.broadcasted_iota(jnp.int32, (rank, rank), 1)
    )
    row_eig = jnp.sum(jnp.where(eye, jnp.broadcast_to(eig_g[...], (rank, rank)), 0.0), 1, keepdims=True)
    whitened = turned / (row_eig * eig_a[...])
    precond = dot(dot(rot_g, whitened, nn), rot_a, nt).astype(BF16).astype(F32)
    total = jnp.zeros((train_ref.shape[0], rank), F32)
    for i in range(rank):
        total = total + train_ref[:, i * rank:(i + 1) * rank].astype(F32) * precond[i:i + 1, :]
    out[...] = dot(jnp.ones((out.shape[0], rank), F32), total, nt)


def body(acts, grads_out, proj_in, proj_out, basis_a, basis_g, eig_a, eig_g, train_grads):
    tokens = acts.shape[1] * lax.axis_size(CTX)
    n_layer = lax.axis_size(LAYER)
    n_y, n_z = lax.axis_size("y"), lax.axis_size("zlo")
    depth, rank = proj_in.shape[1:]
    line_blocks = 2 * n_z
    part = 5 * line_blocks // 8
    local, local_g = acts[0], grads_out[0]
    n_tok = local.shape[0]
    hbm = pl.BlockSpec(memory_space=pltpu.HBM)
    here = jnp.stack(
        [lax.axis_index("y"), lax.axis_index("core"), jnp.int32(n_y), jnp.int32(line_blocks)]
    ).astype(jnp.int32)

    def call(kernel, shape, in_specs, *args, grant=20 << 20, **more):
        return pl.pallas_call(
            kernel,
            out_shape=shape,
            in_specs=in_specs,
            out_specs=jax.tree.map(lambda _: VMEM, shape),
            compiler_params=pltpu.CompilerParams(vmem_limit_bytes=grant),
            **more,
        )(*args)

    def shape(*dims, dtype=BF16):
        return jax.ShapeDtypeStruct(dims, dtype)

    def all_to_all(x, axis):
        return lax.all_to_all(x, axis, 0, 0, tiled=True)

    def permute(x, axis, step):
        size = lax.axis_size(axis)
        return lax.ppermute(x, axis, [(i, (i + step) % size) for i in range(size)])

    both = call(pack, shape(n_z, 2, depth, rank), [VMEM] * 2, proj_in[0], proj_out[0], grant=None)
    line = all_to_all(both.reshape(line_blocks, depth, rank), ("zlo", "core"))
    send = call(
        deal, shape(*local.shape), [SMEM, hbm, hbm], here, local, local_g,
        scratch_shapes=[pltpu.SemaphoreType.DMA],
    )
    got = permute(send, "core", 1)

    low, high = line[:part], line[part:]
    below_low = permute(low, "y", 1)
    above_high = permute(high, "y", -1)
    below_high = permute(high, "y", 1)
    above_low = permute(low, "y", -1)
    far_low = permute(below_low, "y", 1)
    far_high = permute(above_high, "y", -1)

    below, above, far = n_y - 1, 1, n_y // 2
    near = {(0, 0): line, (below, 0): below_low, (below, part): below_high,
            (above, 0): above_low, (above, part): above_high}
    cost = pl.CostEstimate(
        flops=4 * n_tok * rank * local.shape[1] * 3 // 4, bytes_accessed=6 << 20, transcendentals=0
    )
    acc, ahead = call(
        functools.partial(begin, tuple(near), far),
        (shape(2, n_tok, rank, dtype=F32), shape(2, n_tok, line_blocks * depth)),
        [SMEM] + [VMEM] * (3 + len(near)),
        here, local, local_g, got, *near.values(), cost_estimate=cost,
    )
    mine = call(finish, shape(2, n_tok, rank), [VMEM] * 4, ahead, far_low, far_high, acc)
    grad = call(
        functools.partial(outer, float(tokens)), shape(n_y, rank, rank),
        [SMEM, VMEM, VMEM], here, mine, permute(mine, "core", 1),
    )
    grad = call(add_up, shape(n_z, rank, rank), [VMEM], all_to_all(grad, "y"))
    sent = call(
        score, shape(n_layer, train_grads.shape[1], dtype=F32), [VMEM] * 6,
        all_to_all(grad, "zlo"), basis_a[0], basis_g[0], eig_a, eig_g, train_grads[0],
    )
    return jnp.sum(lax.all_to_all(sent, LAYER, 0, 0), 0)


def solution(mesh):
    devices = mesh.devices.reshape(4, 4, 2, 4, 4)
    fine = Mesh(devices, CTX + LAYER)
    return jax.shard_map(
        body,
        mesh=fine,
        in_specs=(
            P(LAYER, CTX, None),
            P(LAYER, CTX, None),
            P(LAYER, CTX, None),
            P(LAYER, CTX, None),
            P(LAYER, None, None),
            P(LAYER, None, None),
            P(LAYER, None),
            P(LAYER, None),
            P(LAYER, CTX, None),
        ),
        out_specs=P(CTX),
        check_vma=False,
    )
```

```python
import functools

import jax
import jax.numpy as jnp
from jax import lax
from jax.experimental import pallas as pl
from jax.experimental.pallas import tpu as pltpu
from jax.sharding import Mesh, PartitionSpec as P


F32 = jnp.float32
BF16 = jnp.bfloat16
HIGHEST = lax.Precision.HIGHEST

CTX = ("y", "zlo", "core")
LAYER = ("zhi", "x")
VMEM = pl.BlockSpec(memory_space=pltpu.VMEM)
SMEM = pl.BlockSpec(memory_space=pltpu.SMEM)


def pack(in_ref, out_ref, out, sems):
    copies = [
        pltpu.make_async_copy(rows, out.at[k, j], sems.at[k, j])
        for k in range(out.shape[0])
        for j, rows in enumerate((in_ref, out_ref))
    ]
    for copy in copies:
        copy.start()
    for copy in copies:
        copy.wait()


def deal(here_ref, acts_ref, grads_ref, send_ref, sem):
    @pl.when(here_ref[1] == 0)
    def _():
        copy = pltpu.make_async_copy(grads_ref, send_ref, sem)
        copy.start()
        copy.wait()

    @pl.when(here_ref[1] != 0)
    def _():
        copy = pltpu.make_async_copy(acts_ref, send_ref, sem)
        copy.start()
        copy.wait()


def products(pieces, here_ref, acts_ref, grads_ref, got_ref, row_refs, mine, other):
    even = here_ref[1] == 0
    for (step, first), rows_ref in zip(pieces, row_refs):
        count, depth, _ = rows_ref.shape
        line = lax.rem(here_ref[0] + step, here_ref[2]) * here_ref[3]
        for k in range(count):
            cols = pl.ds(pl.multiple_of((line + (first + k)) * depth, depth), depth)
            keep = jnp.where(even, acts_ref[:, cols], grads_ref[:, cols])
            mine = mine + jnp.dot(keep, rows_ref[k], preferred_element_type=F32)
            other = other + jnp.dot(got_ref[:, cols], rows_ref[k], preferred_element_type=F32)
    return mine, other


def begin(pieces, later, here_ref, acts_ref, grads_ref, got_ref, *refs):
    rows, (out, ahead) = refs[:-2], refs[-2:]
    zero = jnp.zeros(out.shape[1:], F32)
    out[0], out[1] = products(
        pieces, here_ref, acts_ref, grads_ref, got_ref, rows, zero, zero
    )
    depth = rows[0].shape[1]
    done = 0
    for step, first, count in later:
        line = lax.rem(here_ref[0] + step, here_ref[2]) * here_ref[3]
        cols = pl.ds(pl.multiple_of((line + first) * depth, depth), count * depth)
        put = pl.ds(done * depth, count * depth)
        ahead[0, :, put] = jnp.where(here_ref[1] == 0, acts_ref[:, cols], grads_ref[:, cols])
        ahead[1, :, put] = got_ref[:, cols]
        done += count


def finish(ahead_ref, acc_ref, *refs):
    rows, out = refs[:-1], refs[-1]
    mine, other = acc_ref[0], acc_ref[1]
    done = 0
    for rows_ref in rows:
        depth = rows_ref.shape[1]
        for k in range(rows_ref.shape[0]):
            cols = pl.ds((done + k) * depth, depth)
            mine = mine + jnp.dot(ahead_ref[0, :, cols], rows_ref[k], preferred_element_type=F32)
            other = other + jnp.dot(ahead_ref[1, :, cols], rows_ref[k], preferred_element_type=F32)
        done += rows_ref.shape[0]
    out[0], out[1] = mine.astype(out.dtype), other.astype(out.dtype)


def outer(tokens, here_ref, mine_ref, got_ref, out):
    even = here_ref[1] == 0
    total = jnp.zeros(out.shape[1:], F32)
    for k in range(2):
        mine, got = mine_ref[k].astype(F32), got_ref[1 - k].astype(F32)
        proj_g = jnp.where(even, got, mine).astype(BF16)
        proj_a = jnp.where(even, mine, got).astype(BF16)
        total = total + lax.dot_general(
            proj_g, proj_a, (((0,), (0,)), ((), ())), preferred_element_type=F32
        )
    total = (total / tokens).astype(out.dtype)
    for k in range(out.shape[0]):
        out[k] = total


def add_up(parts_ref, out):
    total = parts_ref[0].astype(F32)
    for k in range(1, parts_ref.shape[0]):
        total = total + parts_ref[k].astype(F32)
    total = total.astype(out.dtype)
    for k in range(out.shape[0]):
        out[k] = total


def score(parts_ref, basis_a, basis_g, eig_a, eig_g, train_ref, out):
    grad = parts_ref[0].astype(F32)
    for k in range(1, parts_ref.shape[0]):
        grad = grad + parts_ref[k].astype(F32)
    rot_a, rot_g = basis_a[...], basis_g[...]
    dot = functools.partial(
        lax.dot_general, precision=HIGHEST, preferred_element_type=F32
    )
    nn, tn, nt = (((1,), (0,)), ((), ())), (((0,), (0,)), ((), ())), (((1,), (1,)), ((), ()))
    turned = dot(dot(rot_g, grad, tn), rot_a, nn)
    rank = turned.shape[0]
    eye = (
        lax.broadcasted_iota(jnp.int32, (rank, rank), 0)
        == lax.broadcasted_iota(jnp.int32, (rank, rank), 1)
    )
    row_eig = jnp.sum(jnp.where(eye, jnp.broadcast_to(eig_g[...], (rank, rank)), 0.0), 1, keepdims=True)
    whitened = turned / (row_eig * eig_a[...])
    precond = dot(dot(rot_g, whitened, nn), rot_a, nt).astype(BF16).astype(F32)
    total = jnp.zeros((train_ref.shape[0], rank), F32)
    for i in range(rank):
        total = total + train_ref[:, i * rank:(i + 1) * rank].astype(F32) * precond[i:i + 1, :]
    out[...] = dot(jnp.ones((out.shape[0], rank), F32), total, nt)


def body(acts, grads_out, proj_in, proj_out, basis_a, basis_g, eig_a, eig_g, train_grads):
    tokens = acts.shape[1] * lax.axis_size(CTX)
    n_layer = lax.axis_size(LAYER)
    n_y, n_z = lax.axis_size("y"), lax.axis_size("zlo")
    depth, rank = proj_in.shape[1:]
    line_blocks = 2 * n_z
    part = 5 * line_blocks // 8
    local, local_g = acts[0], grads_out[0]
    n_tok = local.shape[0]
    hbm = pl.BlockSpec(memory_space=pltpu.HBM)
    here = jnp.stack(
        [lax.axis_index("y"), lax.axis_index("core"), jnp.int32(n_y), jnp.int32(line_blocks)]
    ).astype(jnp.int32)

    def call(kernel, shape, in_specs, *args, grant=20 << 20, **more):
        return pl.pallas_call(
            kernel,
            out_shape=shape,
            in_specs=in_specs,
            compiler_params=pltpu.CompilerParams(vmem_limit_bytes=grant),
            **({"out_specs": jax.tree.map(lambda _: VMEM, shape)} | more),
        )(*args)

    def shape(*dims, dtype=BF16):
        return jax.ShapeDtypeStruct(dims, dtype)

    def all_to_all(x, axis):
        return lax.all_to_all(x, axis, 0, 0, tiled=True)

    def permute(x, axis, step):
        size = lax.axis_size(axis)
        return lax.ppermute(x, axis, [(i, (i + step) % size) for i in range(size)])

    both = call(pack, shape(n_z, 2, depth, rank), [VMEM] * 2,
                proj_in[0], proj_out[0], grant=None, out_specs=pl.BlockSpec(memory_space=pl.ANY),
                scratch_shapes=[pltpu.SemaphoreType.DMA((n_z, 2))])
    line = all_to_all(both.reshape(line_blocks, depth, rank), ("zlo", "core"))
    send = call(
        deal, shape(*local.shape), [SMEM, hbm, hbm], here, local, local_g,
        scratch_shapes=[pltpu.SemaphoreType.DMA],
    )
    got = permute(send, "core", 1)

    low, high = line[:part], line[part:]
    below_low = permute(low, "y", 1)
    above_high = permute(high, "y", -1)
    below_high = permute(high, "y", 1)
    above_low = permute(low, "y", -1)
    far_low = permute(below_low, "y", 1)
    far_high = permute(above_high, "y", -1)

    below, above, far = n_y - 1, 1, n_y // 2
    near = {(0, 0): line, (below, 0): below_low, (above, part): above_high, (below, part): below_high}
    later = ((above, 0, part), (far, 0, line_blocks))
    last = (above_low, far_low, far_high)
    cost = pl.CostEstimate(
        flops=4 * n_tok * rank * local.shape[1] * 5 // 8, bytes_accessed=6 << 20, transcendentals=0
    )
    acc, ahead = call(
        functools.partial(begin, tuple(near), later),
        (shape(2, n_tok, rank, dtype=F32),
         shape(2, n_tok, sum(count for _, _, count in later) * depth)),
        [SMEM] + [VMEM] * (3 + len(near)),
        here, local, local_g, got, *near.values(), cost_estimate=cost,
    )
    mine = call(finish, shape(2, n_tok, rank), [VMEM] * (2 + len(last)), ahead, acc, *last)
    grad = call(
        functools.partial(outer, float(tokens)), shape(n_y, rank, rank),
        [SMEM, VMEM, VMEM], here, mine, permute(mine, "core", 1),
    )
    grad = call(add_up, shape(n_z, rank, rank), [VMEM], all_to_all(grad, "y"))
    sent = call(
        score, shape(n_layer, train_grads.shape[1], dtype=F32), [VMEM] * 6,
        all_to_all(grad, "zlo"), basis_a[0], basis_g[0], eig_a, eig_g, train_grads[0],
    )
    return jnp.sum(lax.all_to_all(sent, LAYER, 0, 0), 0)


def solution(mesh):
    devices = mesh.devices.reshape(4, 4, 2, 4, 4)
    fine = Mesh(devices, CTX + LAYER)
    return jax.shard_map(
        body,
        mesh=fine,
        in_specs=(
            P(LAYER, CTX, None),
            P(LAYER, CTX, None),
            P(LAYER, CTX, None),
            P(LAYER, CTX, None),
            P(LAYER, None, None),
            P(LAYER, None, None),
            P(LAYER, None),
            P(LAYER, None),
            P(LAYER, CTX, None),
        ),
        out_specs=P(CTX),
        check_vma=False,
    )
```

```python
import functools

import jax
import jax.numpy as jnp
from jax import lax
from jax.experimental import pallas as pl
from jax.experimental.pallas import tpu as pltpu
from jax.sharding import Mesh, PartitionSpec as P


F32 = jnp.float32
BF16 = jnp.bfloat16
HIGHEST = lax.Precision.HIGHEST

CTX = ("y", "zlo", "core")
LAYER = ("zhi", "x")
VMEM = pl.BlockSpec(memory_space=pltpu.VMEM)
SMEM = pl.BlockSpec(memory_space=pltpu.SMEM)


def pack(in_ref, out_ref, out, sems):
    copies = [
        pltpu.make_async_copy(rows, out.at[k, j], sems.at[k, j])
        for k in range(out.shape[0])
        for j, rows in enumerate((in_ref, out_ref))
    ]
    for copy in copies:
        copy.start()
    for copy in copies:
        copy.wait()


def deal(here_ref, acts_ref, grads_ref, send_ref, sem):
    @pl.when(here_ref[1] == 0)
    def _():
        copy = pltpu.make_async_copy(grads_ref, send_ref, sem)
        copy.start()
        copy.wait()

    @pl.when(here_ref[1] != 0)
    def _():
        copy = pltpu.make_async_copy(acts_ref, send_ref, sem)
        copy.start()
        copy.wait()


def line_of(here_ref, step):
    y, core, n_y, line_blocks = (here_ref[k] for k in range(4))
    return lax.rem(y + jnp.where(core == 0, step, n_y - step), n_y) * line_blocks


def products(pieces, here_ref, acts_ref, grads_ref, got_ref, row_refs, mine, other):
    even = here_ref[1] == 0
    for (step, first), rows_ref in zip(pieces, row_refs):
        count, depth, _ = rows_ref.shape
        line = line_of(here_ref, step)
        for k in range(count):
            cols = pl.ds(pl.multiple_of((line + (first + k)) * depth, depth), depth)
            keep = jnp.where(even, acts_ref[:, cols], grads_ref[:, cols])
            mine = mine + jnp.dot(keep, rows_ref[k], preferred_element_type=F32)
            other = other + jnp.dot(got_ref[:, cols], rows_ref[k], preferred_element_type=F32)
    return mine, other


def begin(pieces, later, here_ref, acts_ref, grads_ref, got_ref, *refs):
    rows, (out, ahead) = refs[:-2], refs[-2:]
    zero = jnp.zeros(out.shape[1:], F32)
    out[0], out[1] = products(
        pieces, here_ref, acts_ref, grads_ref, got_ref, rows, zero, zero
    )
    depth = rows[0].shape[1]
    done = 0
    for step, first, count in later:
        line = line_of(here_ref, step)
        cols = pl.ds(pl.multiple_of((line + first) * depth, depth), count * depth)
        put = pl.ds(done * depth, count * depth)
        ahead[0, :, put] = jnp.where(here_ref[1] == 0, acts_ref[:, cols], grads_ref[:, cols])
        ahead[1, :, put] = got_ref[:, cols]
        done += count


def finish(ahead_ref, acc_ref, *refs):
    rows, out = refs[:-1], refs[-1]
    mine, other = acc_ref[0], acc_ref[1]
    done = 0
    for rows_ref in rows:
        depth = rows_ref.shape[1]
        for k in range(rows_ref.shape[0]):
            cols = pl.ds((done + k) * depth, depth)
            mine = mine + jnp.dot(ahead_ref[0, :, cols], rows_ref[k], preferred_element_type=F32)
            other = other + jnp.dot(ahead_ref[1, :, cols], rows_ref[k], preferred_element_type=F32)
        done += rows_ref.shape[0]
    out[0], out[1] = mine.astype(out.dtype), other.astype(out.dtype)


def outer(tokens, here_ref, mine_ref, got_ref, out):
    even = here_ref[1] == 0
    total = jnp.zeros(out.shape[1:], F32)
    for k in range(2):
        mine, got = mine_ref[k].astype(F32), got_ref[1 - k].astype(F32)
        proj_g = jnp.where(even, got, mine).astype(BF16)
        proj_a = jnp.where(even, mine, got).astype(BF16)
        total = total + lax.dot_general(
            proj_g, proj_a, (((0,), (0,)), ((), ())), preferred_element_type=F32
        )
    total = (total / tokens).astype(out.dtype)
    for k in range(out.shape[0]):
        out[k] = total


def add_up(parts_ref, out):
    total = parts_ref[0].astype(F32)
    for k in range(1, parts_ref.shape[0]):
        total = total + parts_ref[k].astype(F32)
    total = total.astype(out.dtype)
    for k in range(out.shape[0]):
        out[k] = total


def score(parts_ref, basis_a, basis_g, eig_a, eig_g, train_ref, out):
    grad = parts_ref[0].astype(F32)
    for k in range(1, parts_ref.shape[0]):
        grad = grad + parts_ref[k].astype(F32)
    rot_a, rot_g = basis_a[...], basis_g[...]
    dot = functools.partial(
        lax.dot_general, precision=HIGHEST, preferred_element_type=F32
    )
    nn, tn, nt = (((1,), (0,)), ((), ())), (((0,), (0,)), ((), ())), (((1,), (1,)), ((), ()))
    turned = dot(dot(rot_g, grad, tn), rot_a, nn)
    rank = turned.shape[0]
    eye = (
        lax.broadcasted_iota(jnp.int32, (rank, rank), 0)
        == lax.broadcasted_iota(jnp.int32, (rank, rank), 1)
    )
    row_eig = jnp.sum(jnp.where(eye, jnp.broadcast_to(eig_g[...], (rank, rank)), 0.0), 1, keepdims=True)
    whitened = turned / (row_eig * eig_a[...])
    precond = dot(dot(rot_g, whitened, nn), rot_a, nt).astype(BF16).astype(F32)
    total = jnp.zeros((train_ref.shape[0], rank), F32)
    for i in range(rank):
        total = total + train_ref[:, i * rank:(i + 1) * rank].astype(F32) * precond[i:i + 1, :]
    out[...] = dot(jnp.ones((out.shape[0], rank), F32), total, nt)


def body(acts, grads_out, proj_in, proj_out, basis_a, basis_g, eig_a, eig_g, train_grads):
    tokens = acts.shape[1] * lax.axis_size(CTX)
    n_layer = lax.axis_size(LAYER)
    n_y, n_z = lax.axis_size("y"), lax.axis_size("zlo")
    depth, rank = proj_in.shape[1:]
    line_blocks = 2 * n_z
    part = 3 * line_blocks // 4
    local, local_g = acts[0], grads_out[0]
    n_tok = local.shape[0]
    hbm = pl.BlockSpec(memory_space=pltpu.HBM)
    here = jnp.stack(
        [lax.axis_index("y"), lax.axis_index("core"), jnp.int32(n_y), jnp.int32(line_blocks)]
    ).astype(jnp.int32)

    def call(kernel, shape, in_specs, *args, grant=20 << 20, **more):
        return pl.pallas_call(
            kernel,
            out_shape=shape,
            in_specs=in_specs,
            compiler_params=pltpu.CompilerParams(vmem_limit_bytes=grant),
            **({"out_specs": jax.tree.map(lambda _: VMEM, shape)} | more),
        )(*args)

    def shape(*dims, dtype=BF16):
        return jax.ShapeDtypeStruct(dims, dtype)

    def all_to_all(x, axis):
        return lax.all_to_all(x, axis, 0, 0, tiled=True)

    def permute(x, axis, step):
        size = lax.axis_size(axis)
        return lax.ppermute(x, axis, [(i, (i + step) % size) for i in range(size)])

    both = call(pack, shape(n_z, 2, depth, rank), [VMEM] * 2,
                proj_in[0], proj_out[0], grant=None, out_specs=pl.BlockSpec(memory_space=pl.ANY),
                scratch_shapes=[pltpu.SemaphoreType.DMA((n_z, 2))])
    line = all_to_all(both.reshape(line_blocks, depth, rank), ("zlo", "core"))
    send = call(
        deal, shape(*local.shape), [SMEM, hbm, hbm], here, local, local_g,
        scratch_shapes=[pltpu.SemaphoreType.DMA],
    )
    got = permute(send, "core", 1)

    def along_y(x, step):
        moves = [
            (y * 2 + core, (y + (step if core == 0 else -step)) % n_y * 2 + core)
            for y in range(n_y)
            for core in range(2)
        ]
        return lax.ppermute(x, ("y", "core"), moves)

    low, high = line[:part], line[part:]
    behind_low = along_y(low, 1)
    behind_high = along_y(high, 1)
    ahead_high = along_y(high, -1)
    ahead_low = along_y(low, -1)
    far_low = along_y(behind_low, 1)
    far_high = along_y(ahead_high, -1)

    behind, front, far = n_y - 1, 1, n_y // 2
    near = {(0, 0): line, (behind, 0): behind_low, (behind, part): behind_high, (front, part): ahead_high}
    later = ((front, 0, part), (far, 0, line_blocks))
    last = (ahead_low, far_low, far_high)
    cost = pl.CostEstimate(
        flops=4 * n_tok * rank * local.shape[1] * 5 // 8, bytes_accessed=6 << 20, transcendentals=0
    )
    acc, ahead = call(
        functools.partial(begin, tuple(near), later),
        (shape(2, n_tok, rank, dtype=F32),
         shape(2, n_tok, sum(count for _, _, count in later) * depth)),
        [SMEM] + [VMEM] * (3 + len(near)),
        here, local, local_g, got, *near.values(), cost_estimate=cost,
    )
    mine = call(finish, shape(2, n_tok, rank), [VMEM] * (2 + len(last)), ahead, acc, *last)

    def at(y, z, core):
        return (y * n_z + z) * 2 + core

    def exchange(x, core_along_y):
        other = 1 - core_along_y
        groups = [[at(y, z, core_along_y) for y in range(n_y)] for z in range(n_z)]
        groups += [[at(y, z, other) for z in range(n_z)] for y in range(n_y)]
        return lax.all_to_all(x, CTX, 0, 0, axis_index_groups=groups, tiled=True)

    grad = call(
        functools.partial(outer, float(tokens)), shape(n_y, rank, rank),
        [SMEM, VMEM, VMEM], here, mine, permute(mine, "core", 1),
    )
    grad = call(add_up, shape(n_z, rank, rank), [VMEM], exchange(grad, 0))
    sent = call(
        score, shape(n_layer, train_grads.shape[1], dtype=F32), [VMEM] * 6,
        exchange(grad, 1), basis_a[0], basis_g[0], eig_a, eig_g, train_grads[0],
    )
    return jnp.sum(lax.all_to_all(sent, LAYER, 0, 0), 0)


def solution(mesh):
    devices = mesh.devices.reshape(4, 4, 2, 4, 4)
    fine = Mesh(devices, CTX + LAYER)
    return jax.shard_map(
        body,
        mesh=fine,
        in_specs=(
            P(LAYER, CTX, None),
            P(LAYER, CTX, None),
            P(LAYER, CTX, None),
            P(LAYER, CTX, None),
            P(LAYER, None, None),
            P(LAYER, None, None),
            P(LAYER, None),
            P(LAYER, None),
            P(LAYER, CTX, None),
        ),
        out_specs=P(CTX),
        check_vma=False,
    )
```

```python
import functools

import jax
import jax.numpy as jnp
from jax import lax
from jax.experimental import pallas as pl
from jax.experimental.pallas import tpu as pltpu
from jax.sharding import Mesh, PartitionSpec as P


F32 = jnp.float32
BF16 = jnp.bfloat16
HIGHEST = lax.Precision.HIGHEST

CTX = ("y", "zlo", "core")
LAYER = ("zhi", "x")
VMEM = pl.BlockSpec(memory_space=pltpu.VMEM)
SMEM = pl.BlockSpec(memory_space=pltpu.SMEM)


def pack(in_ref, out_ref, out, sems):
    copies = [
        pltpu.make_async_copy(rows, out.at[k, j], sems.at[k, j])
        for k in range(out.shape[0])
        for j, rows in enumerate((in_ref, out_ref))
    ]
    for copy in copies:
        copy.start()
    for copy in copies:
        copy.wait()


def deal(here_ref, acts_ref, grads_ref, send_ref, sem):
    @pl.when(here_ref[1] == 0)
    def _():
        copy = pltpu.make_async_copy(grads_ref, send_ref, sem)
        copy.start()
        copy.wait()

    @pl.when(here_ref[1] != 0)
    def _():
        copy = pltpu.make_async_copy(acts_ref, send_ref, sem)
        copy.start()
        copy.wait()


def line_of(here_ref, step):
    y, core, n_y, line_blocks = (here_ref[k] for k in range(4))
    return lax.rem(y + jnp.where(core == 0, step, n_y - step), n_y) * line_blocks


def products(pieces, here_ref, acts_ref, grads_ref, got_ref, row_refs, mine, other):
    even = here_ref[1] == 0
    for (step, first), rows_ref in zip(pieces, row_refs):
        count, depth, _ = rows_ref.shape
        line = line_of(here_ref, step)
        for k in range(count):
            cols = pl.ds(pl.multiple_of((line + (first + k)) * depth, depth), depth)
            keep = jnp.where(even, acts_ref[:, cols], grads_ref[:, cols])
            mine = mine + jnp.dot(keep, rows_ref[k], preferred_element_type=F32)
            other = other + jnp.dot(got_ref[:, cols], rows_ref[k], preferred_element_type=F32)
    return mine, other


def begin(pieces, later, here_ref, acts_ref, grads_ref, got_ref, *refs):
    rows, (out, ahead) = refs[:-2], refs[-2:]
    zero = jnp.zeros(out.shape[1:], F32)
    out[0], out[1] = products(
        pieces, here_ref, acts_ref, grads_ref, got_ref, rows, zero, zero
    )
    depth = rows[0].shape[1]
    done = 0
    for step, first, count in later:
        line = line_of(here_ref, step)
        cols = pl.ds(pl.multiple_of((line + first) * depth, depth), count * depth)
        put = pl.ds(done * depth, count * depth)
        ahead[0, :, put] = jnp.where(here_ref[1] == 0, acts_ref[:, cols], grads_ref[:, cols])
        ahead[1, :, put] = got_ref[:, cols]
        done += count


def finish(ahead_ref, acc_ref, *refs):
    rows, out = refs[:-1], refs[-1]
    mine, other = acc_ref[0], acc_ref[1]
    done = 0
    for rows_ref in rows:
        depth = rows_ref.shape[1]
        for k in range(rows_ref.shape[0]):
            cols = pl.ds((done + k) * depth, depth)
            mine = mine + jnp.dot(ahead_ref[0, :, cols], rows_ref[k], preferred_element_type=F32)
            other = other + jnp.dot(ahead_ref[1, :, cols], rows_ref[k], preferred_element_type=F32)
        done += rows_ref.shape[0]
    out[0], out[1] = mine.astype(out.dtype), other.astype(out.dtype)


def outer(tokens, here_ref, mine_ref, got_ref, out):
    even = here_ref[1] == 0
    total = jnp.zeros(out.shape[1:], F32)
    for k in range(2):
        mine, got = mine_ref[k].astype(F32), got_ref[1 - k].astype(F32)
        proj_g = jnp.where(even, got, mine).astype(BF16)
        proj_a = jnp.where(even, mine, got).astype(BF16)
        total = total + lax.dot_general(
            proj_g, proj_a, (((0,), (0,)), ((), ())), preferred_element_type=F32
        )
    total = (total / tokens).astype(out.dtype)
    for k in range(out.shape[0]):
        out[k] = total


def add_up(parts_ref, out):
    total = parts_ref[0].astype(F32)
    for k in range(1, parts_ref.shape[0]):
        total = total + parts_ref[k].astype(F32)
    total = total.astype(out.dtype)
    for k in range(out.shape[0]):
        out[k] = total


def score(parts_ref, basis_a, basis_g, eig_a, eig_g, train_ref, out):
    grad = parts_ref[0].astype(F32)
    for k in range(1, parts_ref.shape[0]):
        grad = grad + parts_ref[k].astype(F32)
    rot_a, rot_g = basis_a[...], basis_g[...]
    dot = functools.partial(
        lax.dot_general, precision=HIGHEST, preferred_element_type=F32
    )
    nn, tn, nt = (((1,), (0,)), ((), ())), (((0,), (0,)), ((), ())), (((1,), (1,)), ((), ()))
    turned = dot(dot(rot_g, grad, tn), rot_a, nn)
    rank = turned.shape[0]
    eye = (
        lax.broadcasted_iota(jnp.int32, (rank, rank), 0)
        == lax.broadcasted_iota(jnp.int32, (rank, rank), 1)
    )
    row_eig = jnp.sum(jnp.where(eye, jnp.broadcast_to(eig_g[...], (rank, rank)), 0.0), 1, keepdims=True)
    whitened = turned / (row_eig * eig_a[...])
    precond = dot(dot(rot_g, whitened, nn), rot_a, nt).astype(BF16).astype(F32)
    total = jnp.zeros((train_ref.shape[0], rank), F32)
    for i in range(rank):
        total = total + train_ref[:, i * rank:(i + 1) * rank].astype(F32) * precond[i:i + 1, :]
    for k in range(out.shape[0]):
        out[k] = dot(jnp.ones((1, rank), F32), total, nt)


def body(acts, grads_out, proj_in, proj_out, basis_a, basis_g, eig_a, eig_g, train_grads):
    tokens = acts.shape[1] * lax.axis_size(CTX)
    n_zhi, n_x = lax.axis_size("zhi"), lax.axis_size("x")
    n_train = train_grads.shape[1]
    n_y, n_z = lax.axis_size("y"), lax.axis_size("zlo")
    depth, rank = proj_in.shape[1:]
    line_blocks = 2 * n_z
    part = 5 * line_blocks // 8
    local, local_g = acts[0], grads_out[0]
    n_tok = local.shape[0]
    hbm = pl.BlockSpec(memory_space=pltpu.HBM)
    here = jnp.stack(
        [lax.axis_index("y"), lax.axis_index("core"), jnp.int32(n_y), jnp.int32(line_blocks)]
    ).astype(jnp.int32)

    def call(kernel, shape, in_specs, *args, grant=20 << 20, **more):
        return pl.pallas_call(
            kernel,
            out_shape=shape,
            in_specs=in_specs,
            compiler_params=pltpu.CompilerParams(vmem_limit_bytes=grant),
            **({"out_specs": jax.tree.map(lambda _: VMEM, shape)} | more),
        )(*args)

    def shape(*dims, dtype=BF16):
        return jax.ShapeDtypeStruct(dims, dtype)

    def all_to_all(x, axis):
        return lax.all_to_all(x, axis, 0, 0, tiled=True)

    def permute(x, axis, step):
        size = lax.axis_size(axis)
        return lax.ppermute(x, axis, [(i, (i + step) % size) for i in range(size)])

    both = call(pack, shape(n_z, 2, depth, rank), [VMEM] * 2,
                proj_in[0], proj_out[0], grant=None, out_specs=pl.BlockSpec(memory_space=pl.ANY),
                scratch_shapes=[pltpu.SemaphoreType.DMA((n_z, 2))])
    line = all_to_all(both.reshape(line_blocks, depth, rank), ("zlo", "core"))
    send = call(
        deal, shape(*local.shape), [SMEM, hbm, hbm], here, local, local_g,
        scratch_shapes=[pltpu.SemaphoreType.DMA],
    )
    got = permute(send, "core", 1)

    def along_y(x, step):
        moves = [
            (y * 2 + core, (y + (step if core == 0 else -step)) % n_y * 2 + core)
            for y in range(n_y)
            for core in range(2)
        ]
        return lax.ppermute(x, ("y", "core"), moves)

    low, high = line[:part], line[part:]
    behind_low = along_y(low, 1)
    behind_high = along_y(high, 1)
    ahead_high = along_y(high, -1)
    ahead_low = along_y(low, -1)
    far_low = along_y(behind_low, 1)
    far_high = along_y(ahead_high, -1)

    behind, front, far = n_y - 1, 1, n_y // 2
    near = {(0, 0): line, (behind, 0): behind_low, (behind, part): behind_high, (front, part): ahead_high}
    later = ((front, 0, part), (far, 0, line_blocks))
    last = (ahead_low, far_low, far_high)
    cost = pl.CostEstimate(
        flops=4 * n_tok * rank * local.shape[1] * 5 // 8, bytes_accessed=6 << 20, transcendentals=0
    )
    acc, ahead = call(
        functools.partial(begin, tuple(near), later),
        (shape(2, n_tok, rank, dtype=F32),
         shape(2, n_tok, sum(count for _, _, count in later) * depth)),
        [SMEM] + [VMEM] * (3 + len(near)),
        here, local, local_g, got, *near.values(), cost_estimate=cost,
    )
    mine = call(finish, shape(2, n_tok, rank), [VMEM] * (2 + len(last)), ahead, acc, *last)
    grad = call(
        functools.partial(outer, float(tokens)), shape(n_y, rank, rank),
        [SMEM, VMEM, VMEM], here, mine, permute(mine, "core", 1),
    )
    grad = call(add_up, shape(n_z, rank, rank), [VMEM], all_to_all(grad, "y"))
    sent = call(
        score, shape(n_zhi, 1, n_train, dtype=F32), [VMEM] * 6,
        all_to_all(grad, "zlo"), basis_a[0], basis_g[0], eig_a, eig_g, train_grads[0],
    )
    sent = call(
        add_up, shape(n_x, 1, n_train, dtype=F32), [VMEM],
        all_to_all(sent, "zhi"),
    )
    return jnp.sum(all_to_all(sent, "x"), (0, 1))


def solution(mesh):
    devices = mesh.devices.reshape(4, 4, 2, 4, 4)
    fine = Mesh(devices, CTX + LAYER)
    return jax.shard_map(
        body,
        mesh=fine,
        in_specs=(
            P(LAYER, CTX, None),
            P(LAYER, CTX, None),
            P(LAYER, CTX, None),
            P(LAYER, CTX, None),
            P(LAYER, None, None),
            P(LAYER, None, None),
            P(LAYER, None),
            P(LAYER, None),
            P(LAYER, CTX, None),
        ),
        out_specs=P(CTX),
        check_vma=False,
    )
```

```python
import functools

import jax
import jax.numpy as jnp
from jax import lax
from jax.experimental import pallas as pl
from jax.experimental.pallas import tpu as pltpu
from jax.sharding import Mesh, PartitionSpec as P


F32 = jnp.float32
BF16 = jnp.bfloat16
HIGHEST = lax.Precision.HIGHEST

CTX = ("y", "zlo", "core")
LAYER = ("zhi", "x")
VMEM = pl.BlockSpec(memory_space=pltpu.VMEM)
SMEM = pl.BlockSpec(memory_space=pltpu.SMEM)


def pack(in_ref, out_ref, out, sems):
    copies = [
        pltpu.make_async_copy(rows, out.at[k, j], sems.at[k, j])
        for k in range(out.shape[0])
        for j, rows in enumerate((in_ref, out_ref))
    ]
    for copy in copies:
        copy.start()
    for copy in copies:
        copy.wait()


def deal(here_ref, acts_ref, grads_ref, send_ref, sem):
    @pl.when(here_ref[1] == 0)
    def _():
        copy = pltpu.make_async_copy(grads_ref, send_ref, sem)
        copy.start()
        copy.wait()

    @pl.when(here_ref[1] != 0)
    def _():
        copy = pltpu.make_async_copy(acts_ref, send_ref, sem)
        copy.start()
        copy.wait()


def line_of(here_ref, step):
    y, core, n_y, line_blocks = (here_ref[k] for k in range(4))
    return lax.rem(y + jnp.where(core == 0, step, n_y - step), n_y) * line_blocks


def products(pieces, here_ref, acts_ref, grads_ref, got_ref, row_refs, mine, other):
    even = here_ref[1] == 0
    for (step, first), rows_ref in zip(pieces, row_refs):
        count, depth, _ = rows_ref.shape
        line = line_of(here_ref, step)
        for k in range(count):
            cols = pl.ds(pl.multiple_of((line + (first + k)) * depth, depth), depth)
            keep = jnp.where(even, acts_ref[:, cols], grads_ref[:, cols])
            mine = mine + jnp.dot(keep, rows_ref[k], preferred_element_type=F32)
            other = other + jnp.dot(got_ref[:, cols], rows_ref[k], preferred_element_type=F32)
    return mine, other


def begin(pieces, later, here_ref, acts_ref, grads_ref, got_ref, *refs):
    rows, (out, ahead) = refs[:-2], refs[-2:]
    zero = jnp.zeros(out.shape[1:], F32)
    out[0], out[1] = products(
        pieces, here_ref, acts_ref, grads_ref, got_ref, rows, zero, zero
    )
    depth = rows[0].shape[1]
    done = 0
    for step, first, count in later:
        line = line_of(here_ref, step)
        cols = pl.ds(pl.multiple_of((line + first) * depth, depth), count * depth)
        put = pl.ds(done * depth, count * depth)
        ahead[0, :, put] = jnp.where(here_ref[1] == 0, acts_ref[:, cols], grads_ref[:, cols])
        ahead[1, :, put] = got_ref[:, cols]
        done += count


def finish(ahead_ref, acc_ref, *refs):
    rows, out = refs[:-1], refs[-1]
    mine, other = acc_ref[0], acc_ref[1]
    done = 0
    for rows_ref in rows:
        depth = rows_ref.shape[1]
        for k in range(rows_ref.shape[0]):
            cols = pl.ds((done + k) * depth, depth)
            mine = mine + jnp.dot(ahead_ref[0, :, cols], rows_ref[k], preferred_element_type=F32)
            other = other + jnp.dot(ahead_ref[1, :, cols], rows_ref[k], preferred_element_type=F32)
        done += rows_ref.shape[0]
    out[0], out[1] = mine.astype(out.dtype), other.astype(out.dtype)


def outer(tokens, here_ref, mine_ref, got_ref, out):
    even = here_ref[1] == 0
    rank = out.shape[2]
    total = jnp.zeros((rank, rank), F32)
    for k in range(2):
        mine, got = mine_ref[k].astype(F32), got_ref[1 - k].astype(F32)
        proj_g = jnp.where(even, got, mine).astype(BF16)
        proj_a = jnp.where(even, mine, got).astype(BF16)
        total = total + lax.dot_general(
            proj_g, proj_a, (((0,), (0,)), ((), ())), preferred_element_type=F32
        )
    total = (total / tokens).astype(out.dtype)
    half = jnp.where(even, total[:out.shape[1]], total[out.shape[1]:])
    for k in range(out.shape[0]):
        out[k] = half


def add_up(parts_ref, out):
    total = parts_ref[0].astype(F32)
    for k in range(1, parts_ref.shape[0]):
        total = total + parts_ref[k].astype(F32)
    out[...] = total


def score(here_ref, mine_ref, got_ref, basis_a, basis_g, eig_a, eig_g, train_ref, out):
    even = here_ref[1] == 0
    mine, got = mine_ref[...], got_ref[...]
    grad = jnp.concatenate([jnp.where(even, mine, got), jnp.where(even, got, mine)], 0)
    rot_a, rot_g = basis_a[...], basis_g[...]
    dot = functools.partial(
        lax.dot_general, precision=HIGHEST, preferred_element_type=F32
    )
    nn, tn, nt = (((1,), (0,)), ((), ())), (((0,), (0,)), ((), ())), (((1,), (1,)), ((), ()))
    turned = dot(dot(rot_g, grad, tn), rot_a, nn)
    rank = turned.shape[0]
    eye = (
        lax.broadcasted_iota(jnp.int32, (rank, rank), 0)
        == lax.broadcasted_iota(jnp.int32, (rank, rank), 1)
    )
    row_eig = jnp.sum(jnp.where(eye, jnp.broadcast_to(eig_g[...], (rank, rank)), 0.0), 1, keepdims=True)
    whitened = turned / (row_eig * eig_a[...])
    precond = dot(dot(rot_g, whitened, nn), rot_a, nt).astype(BF16).astype(F32)
    total = jnp.zeros((train_ref.shape[0], rank), F32)
    for i in range(rank):
        total = total + train_ref[:, i * rank:(i + 1) * rank].astype(F32) * precond[i:i + 1, :]
    out[...] = dot(jnp.ones((out.shape[0], rank), F32), total, nt)


def body(acts, grads_out, proj_in, proj_out, basis_a, basis_g, eig_a, eig_g, train_grads):
    tokens = acts.shape[1] * lax.axis_size(CTX)
    n_layer = lax.axis_size(LAYER)
    n_y, n_z = lax.axis_size("y"), lax.axis_size("zlo")
    depth, rank = proj_in.shape[1:]
    line_blocks = 2 * n_z
    part = 5 * line_blocks // 8
    local, local_g = acts[0], grads_out[0]
    n_tok = local.shape[0]
    hbm = pl.BlockSpec(memory_space=pltpu.HBM)
    here = jnp.stack(
        [lax.axis_index("y"), lax.axis_index("core"), jnp.int32(n_y), jnp.int32(line_blocks)]
    ).astype(jnp.int32)

    def call(kernel, shape, in_specs, *args, grant=20 << 20, **more):
        return pl.pallas_call(
            kernel,
            out_shape=shape,
            in_specs=in_specs,
            compiler_params=pltpu.CompilerParams(vmem_limit_bytes=grant),
            **({"out_specs": jax.tree.map(lambda _: VMEM, shape)} | more),
        )(*args)

    def shape(*dims, dtype=BF16):
        return jax.ShapeDtypeStruct(dims, dtype)

    def all_to_all(x, axis):
        return lax.all_to_all(x, axis, 0, 0, tiled=True)

    def permute(x, axis, step):
        size = lax.axis_size(axis)
        return lax.ppermute(x, axis, [(i, (i + step) % size) for i in range(size)])

    both = call(pack, shape(n_z, 2, depth, rank), [VMEM] * 2,
                proj_in[0], proj_out[0], grant=None, out_specs=pl.BlockSpec(memory_space=pl.ANY),
                scratch_shapes=[pltpu.SemaphoreType.DMA((n_z, 2))])
    line = all_to_all(both.reshape(line_blocks, depth, rank), ("zlo", "core"))
    send = call(
        deal, shape(*local.shape), [SMEM, hbm, hbm], here, local, local_g,
        scratch_shapes=[pltpu.SemaphoreType.DMA],
    )
    got = permute(send, "core", 1)

    def along_y(x, step):
        moves = [
            (y * 2 + core, (y + (step if core == 0 else -step)) % n_y * 2 + core)
            for y in range(n_y)
            for core in range(2)
        ]
        return lax.ppermute(x, ("y", "core"), moves)

    low, high = line[:part], line[part:]
    behind_low = along_y(low, 1)
    behind_high = along_y(high, 1)
    ahead_high = along_y(high, -1)
    ahead_low = along_y(low, -1)
    far_low = along_y(behind_low, 1)
    far_high = along_y(ahead_high, -1)

    behind, front, far = n_y - 1, 1, n_y // 2
    near = {(0, 0): line, (behind, 0): behind_low, (behind, part): behind_high, (front, part): ahead_high}
    later = ((front, 0, part), (far, 0, line_blocks))
    last = (ahead_low, far_low, far_high)
    cost = pl.CostEstimate(
        flops=4 * n_tok * rank * local.shape[1] * 5 // 8, bytes_accessed=6 << 20, transcendentals=0
    )
    acc, ahead = call(
        functools.partial(begin, tuple(near), later),
        (shape(2, n_tok, rank, dtype=F32),
         shape(2, n_tok, sum(count for _, _, count in later) * depth)),
        [SMEM] + [VMEM] * (3 + len(near)),
        here, local, local_g, got, *near.values(), cost_estimate=cost,
    )
    mine = call(finish, shape(2, n_tok, rank), [VMEM] * (2 + len(last)), ahead, acc, *last)
    parts = call(
        functools.partial(outer, float(tokens)), shape(n_y * n_z, rank // 2, rank),
        [SMEM, VMEM, VMEM], here, mine, permute(mine, "core", 1),
    )
    rows = call(
        add_up, shape(rank // 2, rank, dtype=F32), [VMEM],
        all_to_all(parts, ("y", "zlo")),
    )
    sent = call(
        score, shape(n_layer, train_grads.shape[1], dtype=F32), [SMEM] + [VMEM] * 7,
        here, rows, permute(rows, "core", 1),
        basis_a[0], basis_g[0], eig_a, eig_g, train_grads[0],
    )
    return jnp.sum(lax.all_to_all(sent, LAYER, 0, 0), 0)


def solution(mesh):
    devices = mesh.devices.reshape(4, 4, 2, 4, 4)
    fine = Mesh(devices, CTX + LAYER)
    return jax.shard_map(
        body,
        mesh=fine,
        in_specs=(
            P(LAYER, CTX, None),
            P(LAYER, CTX, None),
            P(LAYER, CTX, None),
            P(LAYER, CTX, None),
            P(LAYER, None, None),
            P(LAYER, None, None),
            P(LAYER, None),
            P(LAYER, None),
            P(LAYER, CTX, None),
        ),
        out_specs=P(CTX),
        check_vma=False,
    )
```

```python
import functools

import jax
import jax.numpy as jnp
from jax import lax
from jax.experimental import pallas as pl
from jax.experimental.pallas import tpu as pltpu
from jax.sharding import Mesh, PartitionSpec as P


F32 = jnp.float32
BF16 = jnp.bfloat16
HIGHEST = lax.Precision.HIGHEST

CTX = ("y", "zlo", "core")
LAYER = ("zhi", "x")
VMEM = pl.BlockSpec(memory_space=pltpu.VMEM)
SMEM = pl.BlockSpec(memory_space=pltpu.SMEM)


def pack(in_ref, out_ref, out, sems):
    copies = [
        pltpu.make_async_copy(rows, out.at[k, j], sems.at[k, j])
        for k in range(out.shape[0])
        for j, rows in enumerate((in_ref, out_ref))
    ]
    for copy in copies:
        copy.start()
    for copy in copies:
        copy.wait()


def deal(here_ref, acts_ref, grads_ref, send_ref, sem):
    @pl.when(here_ref[1] == 0)
    def _():
        copy = pltpu.make_async_copy(grads_ref, send_ref, sem)
        copy.start()
        copy.wait()

    @pl.when(here_ref[1] != 0)
    def _():
        copy = pltpu.make_async_copy(acts_ref, send_ref, sem)
        copy.start()
        copy.wait()


def line_of(here_ref, step):
    y, core, n_y, line_blocks = (here_ref[k] for k in range(4))
    return lax.rem(y + jnp.where(core == 0, step, n_y - step), n_y) * line_blocks


def products(pieces, here_ref, acts_ref, grads_ref, got_ref, row_refs, mine, other):
    even = here_ref[1] == 0
    for (step, first), rows_ref in zip(pieces, row_refs):
        count, depth, _ = rows_ref.shape
        line = line_of(here_ref, step)
        for k in range(count):
            cols = pl.ds(pl.multiple_of((line + (first + k)) * depth, depth), depth)
            keep = jnp.where(even, acts_ref[:, cols], grads_ref[:, cols])
            mine = mine + jnp.dot(keep, rows_ref[k], preferred_element_type=F32)
            other = other + jnp.dot(got_ref[:, cols], rows_ref[k], preferred_element_type=F32)
    return mine, other


def begin(pieces, later, here_ref, acts_ref, grads_ref, got_ref, *refs):
    rows, (out, ahead) = refs[:-2], refs[-2:]
    zero = jnp.zeros(out.shape[1:], F32)
    out[0], out[1] = products(
        pieces, here_ref, acts_ref, grads_ref, got_ref, rows, zero, zero
    )
    depth = rows[0].shape[1]
    done = 0
    for step, first, count in later:
        line = line_of(here_ref, step)
        cols = pl.ds(pl.multiple_of((line + first) * depth, depth), count * depth)
        put = pl.ds(done * depth, count * depth)
        ahead[0, :, put] = jnp.where(here_ref[1] == 0, acts_ref[:, cols], grads_ref[:, cols])
        ahead[1, :, put] = got_ref[:, cols]
        done += count


def finish(ahead_ref, acc_ref, *refs):
    rows, out = refs[:-1], refs[-1]
    mine, other = acc_ref[0], acc_ref[1]
    done = 0
    for rows_ref in rows:
        depth = rows_ref.shape[1]
        for k in range(rows_ref.shape[0]):
            cols = pl.ds((done + k) * depth, depth)
            mine = mine + jnp.dot(ahead_ref[0, :, cols], rows_ref[k], preferred_element_type=F32)
            other = other + jnp.dot(ahead_ref[1, :, cols], rows_ref[k], preferred_element_type=F32)
        done += rows_ref.shape[0]
    out[0], out[1] = mine.astype(out.dtype), other.astype(out.dtype)


def outer(tokens, here_ref, mine_ref, got_ref, out):
    even = here_ref[1] == 0
    total = jnp.zeros(out.shape[1:], F32)
    for k in range(2):
        mine, got = mine_ref[k].astype(F32), got_ref[1 - k].astype(F32)
        proj_g = jnp.where(even, got, mine).astype(BF16)
        proj_a = jnp.where(even, mine, got).astype(BF16)
        total = total + lax.dot_general(
            proj_g, proj_a, (((0,), (0,)), ((), ())), preferred_element_type=F32
        )
    total = (total / tokens).astype(out.dtype)
    for k in range(out.shape[0]):
        out[k] = total


def add_up(parts_ref, out):
    total = parts_ref[0].astype(F32)
    for k in range(1, parts_ref.shape[0]):
        total = total + parts_ref[k].astype(F32)
    total = total.astype(out.dtype)
    for k in range(out.shape[0]):
        out[k] = total


def score(parts_ref, basis_a, basis_g, eig_a, eig_g, train_ref, out):
    grad = parts_ref[0].astype(F32)
    for k in range(1, parts_ref.shape[0]):
        grad = grad + parts_ref[k].astype(F32)
    rot_a, rot_g = basis_a[...], basis_g[...]
    dot = functools.partial(
        lax.dot_general, precision=HIGHEST, preferred_element_type=F32
    )
    nn, tn, nt = (((1,), (0,)), ((), ())), (((0,), (0,)), ((), ())), (((1,), (1,)), ((), ()))
    turned = dot(dot(rot_g, grad, tn), rot_a, nn)
    rank = turned.shape[0]
    eye = (
        lax.broadcasted_iota(jnp.int32, (rank, rank), 0)
        == lax.broadcasted_iota(jnp.int32, (rank, rank), 1)
    )
    row_eig = jnp.sum(jnp.where(eye, jnp.broadcast_to(eig_g[...], (rank, rank)), 0.0), 1, keepdims=True)
    whitened = turned / (row_eig * eig_a[...])
    precond = dot(dot(rot_g, whitened, nn), rot_a, nt).astype(BF16).astype(F32)
    total = jnp.zeros((train_ref.shape[0], rank), F32)
    for i in range(rank):
        total = total + train_ref[:, i * rank:(i + 1) * rank].astype(F32) * precond[i:i + 1, :]
    out[...] = dot(jnp.ones((out.shape[0], rank), F32), total, nt)


def body(acts, grads_out, proj_in, proj_out, basis_a, basis_g, eig_a, eig_g, train_grads):
    tokens = acts.shape[1] * lax.axis_size(CTX)
    n_layer = lax.axis_size(LAYER)
    n_y, n_z = lax.axis_size("y"), lax.axis_size("zlo")
    depth, rank = proj_in.shape[1:]
    line_blocks = 2 * n_z
    part = line_blocks // 2
    local, local_g = acts[0], grads_out[0]
    n_tok = local.shape[0]
    hbm = pl.BlockSpec(memory_space=pltpu.HBM)
    here = jnp.stack(
        [lax.axis_index("y"), lax.axis_index("core"), jnp.int32(n_y), jnp.int32(line_blocks)]
    ).astype(jnp.int32)

    def call(kernel, shape, in_specs, *args, grant=20 << 20, **more):
        return pl.pallas_call(
            kernel,
            out_shape=shape,
            in_specs=in_specs,
            compiler_params=pltpu.CompilerParams(vmem_limit_bytes=grant),
            **({"out_specs": jax.tree.map(lambda _: VMEM, shape)} | more),
        )(*args)

    def shape(*dims, dtype=BF16):
        return jax.ShapeDtypeStruct(dims, dtype)

    def all_to_all(x, axis):
        return lax.all_to_all(x, axis, 0, 0, tiled=True)

    def permute(x, axis, step):
        size = lax.axis_size(axis)
        return lax.ppermute(x, axis, [(i, (i + step) % size) for i in range(size)])

    both = call(pack, shape(n_z, 2, depth, rank), [VMEM] * 2,
                proj_in[0], proj_out[0], grant=None, out_specs=pl.BlockSpec(memory_space=pl.ANY),
                scratch_shapes=[pltpu.SemaphoreType.DMA((n_z, 2))])
    line = all_to_all(both.reshape(line_blocks, depth, rank), ("zlo", "core"))
    send = call(
        deal, shape(*local.shape), [SMEM, hbm, hbm], here, local, local_g,
        scratch_shapes=[pltpu.SemaphoreType.DMA],
    )
    got = permute(send, "core", 1)

    def along_y(x, step):
        moves = [
            (y * 2 + core, (y + (step if core == 0 else -step)) % n_y * 2 + core)
            for y in range(n_y)
            for core in range(2)
        ]
        return lax.ppermute(x, ("y", "core"), moves)

    low, high = line[:part], line[part:]
    behind_low = along_y(low, 1)
    behind_high = along_y(high, 1)
    ahead_high = along_y(high, -1)
    ahead_low = along_y(low, -1)
    far_low = along_y(behind_low, 1)
    far_high = along_y(ahead_high, -1)

    behind, front, far = n_y - 1, 1, n_y // 2
    near = {(0, 0): line, (behind, 0): behind_low, (behind, part): behind_high, (front, part): ahead_high}
    later = ((front, 0, part), (far, 0, line_blocks))
    last = (ahead_low, far_low, far_high)
    cost = pl.CostEstimate(
        flops=4 * n_tok * rank * local.shape[1] * 5 // 8, bytes_accessed=6 << 20, transcendentals=0
    )
    acc, ahead = call(
        functools.partial(begin, tuple(near), later),
        (shape(2, n_tok, rank, dtype=F32),
         shape(2, n_tok, sum(count for _, _, count in later) * depth)),
        [SMEM] + [VMEM] * (3 + len(near)),
        here, local, local_g, got, *near.values(), cost_estimate=cost,
    )
    mine = call(finish, shape(2, n_tok, rank), [VMEM] * (2 + len(last)), ahead, acc, *last)
    grad = call(
        functools.partial(outer, float(tokens)), shape(n_y, rank, rank),
        [SMEM, VMEM, VMEM], here, mine, permute(mine, "core", 1),
    )
    grad = call(add_up, shape(n_z, rank, rank), [VMEM], all_to_all(grad, "y"))
    sent = call(
        score, shape(n_layer, train_grads.shape[1], dtype=F32), [VMEM] * 6,
        all_to_all(grad, "zlo"), basis_a[0], basis_g[0], eig_a, eig_g, train_grads[0],
    )
    return jnp.sum(lax.all_to_all(sent, LAYER, 0, 0), 0)


def solution(mesh):
    devices = mesh.devices.reshape(4, 4, 2, 4, 4)
    fine = Mesh(devices, CTX + LAYER)
    return jax.shard_map(
        body,
        mesh=fine,
        in_specs=(
            P(LAYER, CTX, None),
            P(LAYER, CTX, None),
            P(LAYER, CTX, None),
            P(LAYER, CTX, None),
            P(LAYER, None, None),
            P(LAYER, None, None),
            P(LAYER, None),
            P(LAYER, None),
            P(LAYER, CTX, None),
        ),
        out_specs=P(CTX),
        check_vma=False,
    )
```
